32 devices in a mesh: dp: 4 (over y, core), ctx: 8 (over z, x).
Axes of the slice: x: 2, y: 2, z: 4, core: 2. Of those that a mesh axis runs over, the one named last changes fastest.
Arguments:
- queries: bfloat16 [4608, 256], P(('dp', 'ctx')), parts along dimension 0, may hold values from -5 to 5
- keys: bfloat16 [4608, 256], P(('dp', 'ctx')), parts along dimension 0, may hold values from -5 to 5
- values: bfloat16 [4608, 256], P(('dp', 'ctx')), parts along dimension 0, may hold values from -2.5 to 2.5
- out_grad: bfloat16 [4608, 256], P(('dp', 'ctx')), parts along dimension 0, may hold values from -5 to 5
- span_end: int32 [4608], P(('dp', 'ctx')), parts along dimension 0, may hold values from 0 to 1152, as said below
Outputs:
- output: bfloat16 [4608, 256], P(('dp', 'ctx')), parts along dimension 0
- query_grad: float32 [4608, 256], P(('dp', 'ctx')), parts along dimension 0
- key_grad: float32 [4608, 256], P(('dp', 'ctx')), parts along dimension 0
- value_grad: float32 [4608, 256], P(('dp', 'ctx')), parts along dimension 0
The draws below stay inside these ranges and needn't reach their ends.
There are 4 independent parts, one for each index of `dp`. The reference program is written for one: setup_inputs(seed, part) draws one part's arguments, and reference() takes and returns one part's arrays. A program takes and returns all parts, laid end to end along the dimension named above; each array names one. Nothing has to cross between parts.
Inputs may be any that keep to these rules, and one draw needn't show every extreme that they name: `span_end`: image spans are runs of consecutive tokens, each of at most 288 tokens; every token of a span holds the position just past the span's last token; the last 288 tokens of a document form one span.
All inputs are finite; a program needn't handle non-finite values.
Results may differ from the reference program's by a relative error of at most 0.035.
Values may be sent and summed in bfloat16 or wider, within the bound.
A program may use at most 64 MiB of HBM per device.

```python
import math
import jax
import jax.numpy as jnp
from jax import lax

HEADS = 2
HEAD_DIM = 128
FEATURES = 256
TOKENS = 1152
IMG = 288


def draw_queries(key, part):
    width = HEADS * HEAD_DIM
    drawn = jnp.clip(jax.random.normal(jax.random.fold_in(key, 11), (TOKENS, width), jnp.float32), -4.0, 4.0)
    return drawn.astype(jnp.bfloat16)


def draw_keys(key, part):
    width = HEADS * HEAD_DIM
    drawn = jnp.clip(jax.random.normal(jax.random.fold_in(key, 31), (TOKENS, width), jnp.float32), -4.0, 4.0)
    return drawn.astype(jnp.bfloat16)


def draw_span_end(key, part):
    span_count = TOKENS // (IMG // 2) + 2
    gaps = jax.random.randint(jax.random.fold_in(key, 21), (span_count,), 0, IMG)
    lengths = jax.random.randint(jax.random.fold_in(key, 22), (span_count,), IMG // 2, IMG + 1)
    ends = jnp.cumsum(gaps + lengths)
    starts = ends - lengths
    kept = ends <= TOKENS - IMG - 1
    positions = jnp.arange(TOKENS, dtype=jnp.int32)
    inside = (positions[:, None] >= starts[None, :]) & (positions[:, None] < ends[None, :]) & kept[None, :]
    result = jnp.sum(jnp.where(inside, ends[None, :], 0), axis=1) + jnp.where(positions >= TOKENS - IMG, TOKENS, 0)
    return result.astype(jnp.int32)


def block_levels(stream_key, dims, pieces, smallest, top_value):
    level = 1.0
    for position, shards_of in pieces:
        heights = jax.random.uniform(jax.random.fold_in(jax.random.fold_in(stream_key, 6), position), (shards_of,), jnp.float32, smallest / len(pieces), top_value / len(pieces))
        level = level * jnp.repeat(jnp.exp(heights), dims[position] // shards_of).reshape((-1,) + (1,) * (len(dims) - 1 - position))
    return level


def gaussian(stream_key, extent, scale, limit, cuts=(), kind=jnp.bfloat16):
    entries = jax.random.normal(stream_key, extent, jnp.float32) * scale
    if len(cuts) > 0:
        entries = block_levels(stream_key, extent, cuts, -0.22, 0.18) * entries
    return jnp.clip(entries, min=-limit, max=limit).astype(kind)


def setup_inputs(seed: int = 0, part: int = 0) -> dict:
    arg_keys = jax.random.split(jax.random.key(seed), 6)
    part_splits = jax.random.split(jax.random.fold_in(arg_keys[5], part), 6)
    queries = draw_queries(jax.random.fold_in(jax.random.fold_in(arg_keys[5], part), 71), part)
    keys = draw_keys(jax.random.fold_in(jax.random.fold_in(arg_keys[5], part), 71), part)
    values = gaussian(part_splits[2], (TOKENS, FEATURES), 0.5, 2.5, ((0, 8),))
    out_grad = gaussian(part_splits[3], (TOKENS, FEATURES), 1.0, 5.0, ((0, 8),))
    span_end = draw_span_end(jax.random.fold_in(jax.random.fold_in(arg_keys[5], part), 71), part)
    return {"queries": queries, "keys": keys, "values": values, "out_grad": out_grad, "span_end": span_end}


def rounded(matrix):
    return lax.optimization_barrier(matrix.astype(jnp.bfloat16)).astype(jnp.float32)


def reference(queries, keys, values, out_grad, span_end):
    total_rows = queries.shape[0]
    scaling = HEAD_DIM ** -0.5
    query_all = queries.astype(jnp.float32).reshape(total_rows, HEADS, HEAD_DIM)
    key_all = keys.astype(jnp.float32).reshape(total_rows, HEADS, HEAD_DIM)
    value_all = values.astype(jnp.float32).reshape(total_rows, HEADS, HEAD_DIM)
    grad_all = out_grad.astype(jnp.float32).reshape(total_rows, HEADS, HEAD_DIM)
    positions = jnp.arange(total_rows, dtype=jnp.int32)
    limits = jnp.maximum(positions + 1, span_end.astype(jnp.int32))
    block_rows = math.gcd(512, total_rows)
    block_count = total_rows // block_rows

    def masked_scores(offset):
        query_block = lax.dynamic_slice_in_dim(query_all, offset, block_rows, 0)
        limit_block = lax.dynamic_slice_in_dim(limits, offset, block_rows, 0)
        scores = jnp.einsum("qhd,khd->hqk", query_block, key_all) * scaling
        visible = (positions[None, :] < limit_block[:, None])[None]
        return jnp.where(visible, scores, -jnp.inf)

    def forward_block(index):
        offset = index * block_rows
        scores = masked_scores(offset)
        highest = jnp.max(scores, axis=-1)
        log_total = highest + jnp.log(jnp.sum(jnp.exp(scores - highest[..., None]), axis=-1))
        probs = jnp.exp(scores - log_total[..., None])
        output = jnp.einsum("hqk,khd->qhd", probs, value_all,
                            precision=lax.Precision.HIGHEST).astype(jnp.bfloat16)
        return output, log_total

    indices = jnp.arange(block_count, dtype=jnp.int32)
    outputs, log_totals = lax.map(forward_block, indices)
    output_all = outputs.reshape(total_rows, HEADS, HEAD_DIM)

    def backward_block(totals, index):
        key_grad, value_grad = totals
        offset = index * block_rows
        query_block = lax.dynamic_slice_in_dim(query_all, offset, block_rows, 0)
        grad_block = lax.dynamic_slice_in_dim(grad_all, offset, block_rows, 0)
        output_block = lax.dynamic_slice_in_dim(output_all, offset, block_rows, 0).astype(jnp.float32)
        scores = masked_scores(offset)
        probs = jnp.exp(scores - log_totals[index][..., None])
        row_dot = jnp.sum(grad_block * output_block, axis=-1).T
        prob_grad = jnp.einsum("qhd,khd->hqk", grad_block, value_all)
        score_grad = rounded(probs * (prob_grad - row_dot[..., None]))
        query_grad = jnp.einsum("hqk,khd->qhd", score_grad, key_all) * scaling
        key_grad = key_grad + jnp.einsum("hqk,qhd->khd", score_grad, query_block)
        value_grad = value_grad + jnp.einsum("hqk,qhd->khd", rounded(probs), grad_block)
        return (key_grad, value_grad), query_grad

    zero_rows = jnp.zeros((total_rows, HEADS, HEAD_DIM), jnp.float32)
    grads, query_grads = lax.scan(backward_block, (zero_rows, zero_rows), indices)
    key_grad, value_grad = grads
    flat_shape = (total_rows, HEADS * HEAD_DIM)
    return (output_all.reshape(flat_shape),
            query_grads.reshape(flat_shape),
            (key_grad * scaling).reshape(flat_shape),
            value_grad.reshape(flat_shape))
```

```python
import functools

import jax
import jax.numpy as jnp
from jax import lax
from jax.experimental import pallas as pl
from jax.experimental.pallas import tpu as pltpu
from jax.sharding import PartitionSpec as P

HEADS = 2
HEAD_DIM = 128
IMG = 288
HIDDEN = -1e30
KEY, VALUE, QUERY, GRAD = range(4)


def dot(a, b, a_dim, b_dim):
    return lax.dot_general(a, b, (((a_dim,), (b_dim,)), ((), ())), preferred_element_type=jnp.float32)


def kernel(
    n, rows,
    q_in, k_in, v_in, g_in, lim_ref,
    o_ref, dq_ref, dk_ref, dv_ref,
    buf, limits, st, dp, stats, top, acc_o, acc_q, acc_k, acc_v, res_out, res_in,
    send_sem, recv_sem, lim_send, lim_recv, stat_send, stat_recv, res_send, res_recv,
):
    scaling = HEAD_DIM ** -0.5
    blocks = n // HEADS
    span = HEADS * rows
    cut = blocks * span - IMG
    me = lax.axis_index("ctx")
    z = me // HEADS
    x = me % HEADS
    sources = (k_in, v_in, q_in, g_in)

    def device(index):
        return {"ctx": index}

    def needed(query_block, key_block):
        return (
            (key_block <= query_block)
            | ((query_block + 1) * span > cut)
            | ((key_block <= query_block + 1) & (key_block * span < cut))
        )

    ahead = (z + 1 < blocks) & needed(z, z + 1)
    behind = (z > 0) & needed(z - 1, z)

    barrier = pltpu.get_barrier_semaphore()
    for step in range(1, n):
        pl.semaphore_signal(barrier, inc=1, device_id=device(lax.rem(me + step, n)))
    pl.semaphore_wait(barrier, n - 1)

    own_rows = pl.ds(pl.multiple_of(x * rows, 16), rows)
    other_rows = pl.ds(pl.multiple_of((1 - x) * rows, 16), rows)

    def limit_copy(slot, target, send):
        return pltpu.make_async_remote_copy(
            src_ref=lim_ref, dst_ref=limits.at[slot], send_sem=lim_send.at[send],
            recv_sem=lim_recv.at[slot], device_id=device(target))

    def block_copy(array, target, head):
        return pltpu.make_async_remote_copy(
            src_ref=sources[array].at[:, pl.ds(head * HEAD_DIM, HEAD_DIM)],
            dst_ref=buf.at[array, z, own_rows],
            send_sem=send_sem.at[array, target, head],
            recv_sem=recv_sem.at[array, z, x],
            device_id=device(target * HEADS + head))

    def local_copy(array, target, head):
        return pltpu.make_async_copy(
            sources[array].at[:, pl.ds(head * HEAD_DIM, HEAD_DIM)],
            buf.at[array, z, own_rows],
            recv_sem.at[array, z, x])

    def stat_copy(target):
        return pltpu.make_async_remote_copy(
            src_ref=stats.at[z], dst_ref=stats.at[z], send_sem=stat_send.at[target],
            recv_sem=stat_recv.at[z], device_id=device(target * HEADS + x))

    def result_copy(slot):
        return pltpu.make_async_remote_copy(
            src_ref=res_out.at[slot], dst_ref=res_in.at[slot], send_sem=res_send.at[slot],
            recv_sem=res_recv.at[slot], device_id=device(z * HEADS + 1 - x))

    limit_copy(0, z * HEADS + 1 - x, 0).start()
    @pl.when(ahead)
    def _():
        for head in range(HEADS):
            limit_copy(1 + x, (z + 1) * HEADS + head, 1 + head).start()

    routes = []
    for step in range(blocks):
        for array, target in (
            (KEY, blocks - 1 - step), (VALUE, blocks - 1 - step), (QUERY, step), (GRAD, step)):
            wanted = needed(target, z) if array in (KEY, VALUE) else needed(z, target)
            for head in range(HEADS):
                routes.append((array, target, head, wanted))
    for array, target, head, wanted in routes:
        mine = target * HEADS + head == me
        @pl.when(wanted & mine)
        def _():
            local_copy(array, target, head).start()
        @pl.when(wanted & jnp.logical_not(mine))
        def _():
            block_copy(array, target, head).start()

    def arrive(array, block):
        for portion in range(HEADS):
            ref = buf.at[array, block, pl.ds(portion * rows, rows)]
            pltpu.make_async_copy(ref, ref, recv_sem.at[array, block, portion]).wait()

    for array in (KEY, QUERY, VALUE, GRAD):
        arrive(array, z)
    limit_copy(0, z * HEADS + 1 - x, 0).wait_recv()
    own_limit = jnp.maximum(lim_ref[...], limits[0])
    key_row = lax.broadcasted_iota(jnp.int32, (span, span), 0)
    top[...] = jnp.full_like(top, HIDDEN)

    def score(block, masked):
        if not (masked == "own"):
            arrive(KEY, block)
            arrive(VALUE, block)
        scores = dot(buf[KEY, block], buf[QUERY, z], 1, 1) * scaling
        if masked:
            scores = jnp.where(key_row + block * span < own_limit, scores, HIDDEN)
        st[block] = scores
        dp[block] = dot(buf[VALUE, block], buf[GRAD, z], 1, 1)
        top[...] = jnp.maximum(top[...], jnp.max(scores, axis=0, keepdims=True))

    score(z, "own")
    @pl.when(ahead)
    def _():
        score(z + 1, "ahead")

    @pl.loop(1, z + 1)
    def _(back):
        score(z - back, None)

    last = z + ahead.astype(jnp.int32) + 1
    highest = top[...]

    def total(block, carry):
        sums, dots = carry
        probs = jnp.exp(st[block] - highest)
        st[block] = probs
        return (sums + jnp.sum(probs, axis=0, keepdims=True),
                dots + jnp.sum(probs * dp[block], axis=0, keepdims=True))

    zero = jnp.zeros_like(highest)
    sums, dots = lax.fori_loop(0, last, total, (zero, zero))
    row_dot = dots / sums
    inverse = 1.0 / sums
    stats[z, 0:1] = highest + jnp.log(sums)
    stats[z, 1:2] = row_dot
    for target in range(blocks):
        @pl.when(needed(z, target) & (z != target))
        def _():
            stat_copy(target).start()

    def own_query(block):
        probs = st[block] * inverse
        score_grad = (probs * (dp[block] - row_dot)).astype(jnp.bfloat16)
        return probs.astype(jnp.bfloat16), score_grad

    probs, score_grad = own_query(z)
    acc_o[...] = dot(probs, buf[VALUE, z], 0, 0)
    acc_q[...] = dot(score_grad, buf[KEY, z], 0, 0)
    acc_v[...] = dot(probs, buf[GRAD, z], 1, 0)
    acc_k[...] = dot(score_grad, buf[QUERY, z], 1, 0)

    def add_query(block):
        probs, score_grad = own_query(block)
        acc_o[...] += dot(probs, buf[VALUE, block], 0, 0)
        acc_q[...] += dot(score_grad, buf[KEY, block], 0, 0)

    @pl.when(ahead)
    def _():
        add_query(z + 1)

    @pl.loop(1, z + 1)
    def _(back):
        add_query(z - back)

    res_out[0] = acc_o[other_rows, :].astype(jnp.bfloat16)
    result_copy(0).start()
    res_out[1] = (acc_q[other_rows, :] * scaling).astype(jnp.bfloat16)
    result_copy(1).start()

    def add_key(block, masked):
        arrive(QUERY, block)
        arrive(GRAD, block)
        scores = dot(buf[KEY, z], buf[QUERY, block], 1, 1) * scaling
        if masked:
            limit_copy(1, 0, 1).wait_recv()
            limit_copy(2, 0, 1).wait_recv()
            limit = jnp.maximum(limits[1], limits[2])
            scores = jnp.where(key_row + z * span < limit, scores, HIDDEN)
        prob_grad = dot(buf[VALUE, z], buf[GRAD, block], 1, 1)
        pltpu.make_async_copy(stats.at[block], stats.at[block], stat_recv.at[block]).wait()
        probs = jnp.exp(scores - stats[block, 0:1])
        score_grad = (probs * (prob_grad - stats[block, 1:2])).astype(jnp.bfloat16)
        acc_v[...] += dot(probs.astype(jnp.bfloat16), buf[GRAD, block], 1, 0)
        acc_k[...] += dot(score_grad, buf[QUERY, block], 1, 0)

    @pl.when(behind)
    def _():
        add_key(z - 1, True)

    @pl.loop(z + 1, blocks)
    def _(block):
        add_key(block, False)

    res_out[2] = (acc_k[other_rows, :] * scaling).astype(jnp.bfloat16)
    result_copy(2).start()
    res_out[3] = acc_v[other_rows, :].astype(jnp.bfloat16)
    result_copy(3).start()

    own_columns = pl.ds(pl.multiple_of(x * HEAD_DIM, HEAD_DIM), HEAD_DIM)
    other_columns = pl.ds(pl.multiple_of((1 - x) * HEAD_DIM, HEAD_DIM), HEAD_DIM)
    o_ref[:, own_columns] = acc_o[own_rows, :].astype(jnp.bfloat16)
    dq_ref[:, own_columns] = acc_q[own_rows, :] * scaling
    dk_ref[:, own_columns] = acc_k[own_rows, :] * scaling
    dv_ref[:, own_columns] = acc_v[own_rows, :]
    for slot, ref in enumerate((o_ref, dq_ref, dk_ref, dv_ref)):
        result_copy(slot).wait_recv()
        ref[:, other_columns] = res_in[slot].astype(ref.dtype)

    for slot in range(4):
        result_copy(slot).wait_send()
    limit_copy(0, 0, 0).wait_send()
    @pl.when(ahead)
    def _():
        for head in range(HEADS):
            limit_copy(0, 0, 1 + head).wait_send()
    for target in range(blocks):
        @pl.when(needed(z, target) & (z != target))
        def _():
            stat_copy(target).wait_send()
    for array, target, head, wanted in routes:
        @pl.when(wanted & (target * HEADS + head != me))
        def _():
            block_copy(array, target, head).wait_send()


def solution(mesh):
    n = mesh.shape["ctx"]

    def local(queries, keys, values, out_grad, span_end):
        rows = queries.shape[0]
        blocks, span = n // HEADS, HEADS * rows
        device = lax.axis_index("ctx")
        offset = lax.rem(device, HEADS) * rows
        positions = device * rows + jnp.arange(rows, dtype=jnp.int32)
        limit = jnp.maximum(positions + 1, span_end)
        limit = lax.dynamic_update_slice(jnp.zeros((1, span), jnp.int32), limit[None], (0, offset))
        f32, bf16 = jnp.float32, jnp.bfloat16
        anywhere = pl.BlockSpec(memory_space=pl.ANY)
        vmem = pl.BlockSpec(memory_space=pltpu.VMEM)
        dma = pltpu.SemaphoreType.DMA
        return pl.pallas_call(
            functools.partial(kernel, n, rows),
            out_shape=tuple(
                jax.ShapeDtypeStruct(queries.shape, kind) for kind in (bf16, f32, f32, f32)),
            in_specs=[anywhere] * 4 + [vmem],
            out_specs=(vmem,) * 4,
            scratch_shapes=[
                pltpu.VMEM((4, blocks, span, HEAD_DIM), bf16),
                pltpu.VMEM((3, 1, span), jnp.int32),
                pltpu.VMEM((blocks, span, span), f32),
                pltpu.VMEM((blocks, span, span), f32),
                pltpu.VMEM((blocks, 2, span), f32),
                pltpu.VMEM((1, span), f32),
                pltpu.VMEM((span, HEAD_DIM), f32),
                pltpu.VMEM((span, HEAD_DIM), f32),
                pltpu.VMEM((span, HEAD_DIM), f32),
                pltpu.VMEM((span, HEAD_DIM), f32),
                pltpu.VMEM((4, rows, HEAD_DIM), bf16),
                pltpu.VMEM((4, rows, HEAD_DIM), bf16),
                dma((4, blocks, HEADS)),
                dma((4, blocks, HEADS)),
                dma((3,)),
                dma((3,)),
                dma((blocks,)),
                dma((blocks,)),
                dma((4,)),
                dma((4,)),
            ],
            compiler_params=pltpu.CompilerParams(collective_id=0, has_side_effects=True),
        )(queries, keys, values, out_grad, limit)

    spec = P(("dp", "ctx"), None)
    return jax.shard_map(
        local, mesh=mesh, in_specs=(spec,) * 4 + (P(("dp", "ctx")),),
        out_specs=(spec,) * 4, check_vma=False)
```

```python
import functools

import jax
import jax.numpy as jnp
from jax import lax
from jax.experimental import pallas as pl
from jax.experimental.pallas import tpu as pltpu
from jax.sharding import PartitionSpec as P

HEADS = 2
HEAD_DIM = 128
IMG = 288
DIRECT = 2
HIDDEN = -1e30
KEY, VALUE, QUERY, GRAD = range(4)


def dot(a, b, a_dim, b_dim):
    return lax.dot_general(a, b, (((a_dim,), (b_dim,)), ((), ())), preferred_element_type=jnp.float32)


def kernel(
    n, rows,
    q_in, k_in, v_in, g_in, ends_in,
    o_ref, dq_ref, dk_ref, dv_ref,
    buf, ends, st, dp, st_key, dp_key, stats, top, acc_o, acc_q, acc_k, acc_v, res_out, res_in,
    send_sem, recv_sem, lim_send, lim_recv, stat_send, stat_recv, res_send, res_recv, pass_send, pass_recv,
):
    scaling = HEAD_DIM ** -0.5
    blocks = n // HEADS
    span = HEADS * rows
    cut = blocks * span - IMG
    me = lax.axis_index("ctx")
    z = me // HEADS
    x = me % HEADS
    sources = (k_in, v_in, q_in, g_in)

    def device(index):
        return {"ctx": index}

    def needed(query_block, key_block):
        return (
            (key_block <= query_block)
            | ((query_block + 1) * span > cut)
            | ((key_block <= query_block + 1) & (key_block * span < cut))
        )

    ahead = (z + 1 < blocks) & needed(z, z + 1)
    behind = (z > 0) & needed(z - 1, z)

    barrier = pltpu.get_barrier_semaphore()
    for step in range(1, n):
        pl.semaphore_signal(barrier, inc=1, device_id=device(lax.rem(me + step, n)))
    own_rows = pl.ds(pl.multiple_of(x * rows, 16), rows)
    other_rows = pl.ds(pl.multiple_of((1 - x) * rows, 16), rows)

    own_columns = pl.ds(pl.multiple_of(x * HEAD_DIM, HEAD_DIM), HEAD_DIM)
    other_columns = pl.ds(pl.multiple_of((1 - x) * HEAD_DIM, HEAD_DIM), HEAD_DIM)

    def limit_copy(slot, target, send):
        return pltpu.make_async_remote_copy(
            src_ref=ends_in, dst_ref=ends.at[slot], send_sem=lim_send.at[send],
            recv_sem=lim_recv.at[slot], device_id=device(target))

    def own_limit_copy():
        return pltpu.make_async_copy(ends_in, ends.at[x], lim_recv.at[x])

    def limits(block, slot):
        for portion in range(HEADS):
            ref = ends.at[slot + portion]
            pltpu.make_async_copy(ref, ref, lim_recv.at[slot + portion]).wait()
        joined = jnp.concatenate([ends[slot + portion] for portion in range(HEADS)], axis=1)
        position = lax.broadcasted_iota(jnp.int32, (1, span), 1) + block * span
        return jnp.maximum(position + 1, joined)

    def block_copy(array, target, head):
        return pltpu.make_async_remote_copy(
            src_ref=sources[array].at[:, pl.ds(head * HEAD_DIM, HEAD_DIM)],
            dst_ref=buf.at[array, z, own_rows],
            send_sem=send_sem.at[array, target, head],
            recv_sem=recv_sem.at[array, z, x],
            device_id=device(target * HEADS + head))

    def local_copy(array):
        return pltpu.make_async_copy(
            sources[array].at[:, own_columns],
            buf.at[array, z, own_rows],
            recv_sem.at[array, z, x])

    def stat_copy(target):
        return pltpu.make_async_remote_copy(
            src_ref=stats.at[z], dst_ref=stats.at[z], send_sem=stat_send.at[target],
            recv_sem=stat_recv.at[z], device_id=device(target * HEADS + x))

    def result_copy(slot):
        return pltpu.make_async_remote_copy(
            src_ref=res_out.at[slot], dst_ref=res_in.at[slot], send_sem=res_send.at[slot],
            recv_sem=res_recv.at[slot], device_id=device(z * HEADS + 1 - x))

    own_limit_copy().start()
    for array in range(4):
        local_copy(array).start()
    pl.semaphore_wait(barrier, n - 1)

    limit_copy(x, z * HEADS + 1 - x, 0).start()
    @pl.when(ahead)
    def _():
        for head in range(HEADS):
            limit_copy(HEADS + x, (z + 1) * HEADS + head, 1 + head).start()

    routes = []
    for step in range(blocks):
        for array, target in (
            (KEY, blocks - 1 - step), (VALUE, blocks - 1 - step), (QUERY, step), (GRAD, step)):
            wanted = needed(target, z) if array in (KEY, VALUE) else needed(z, target)
            near = (target - z <= DIRECT) & (z - target <= DIRECT)
            for head in range(HEADS):
                away = target * HEADS + head != me
                routes.append((array, target, head, wanted & near & away))
    for array, target, head, wanted in routes:
        @pl.when(wanted)
        def _():
            block_copy(array, target, head).start()

    def forward_copy(array, block):
        target = z + 1 if array in (KEY, VALUE) else z - 1
        return pltpu.make_async_remote_copy(
            src_ref=buf.at[array, block], dst_ref=buf.at[array, block],
            send_sem=pass_send.at[array, block], recv_sem=pass_recv.at[array, block],
            device_id=device(target * HEADS + x))

    def forwards(array, block):
        if array in (KEY, VALUE):
            return (z - block >= DIRECT) & (z + 1 < blocks)
        return (block - z >= DIRECT) & (z > 0)

    def arrive_direct(array, block):
        for portion in range(HEADS):
            ref = buf.at[array, block, pl.ds(portion * rows, rows)]
            pltpu.make_async_copy(ref, ref, recv_sem.at[array, block, portion]).wait()

    def arrive(arrays, block):
        near = (block - z <= DIRECT) & (z - block <= DIRECT)
        @pl.when(near)
        def _():
            for array in arrays:
                arrive_direct(array, block)
        @pl.when(jnp.logical_not(near))
        def _():
            for array in arrays:
                ref = buf.at[array, block]
                pltpu.make_async_copy(ref, ref, pass_recv.at[array, block]).wait()
        @pl.when(forwards(arrays[0], block))
        def _():
            for array in arrays:
                forward_copy(array, block).start()

    for array in (KEY, QUERY, VALUE, GRAD):
        arrive_direct(array, z)
    own_limit = limits(z, 0)
    key_row = lax.broadcasted_iota(jnp.int32, (span, span), 0)
    top[...] = jnp.full_like(top, HIDDEN)

    def score(block, masked):
        if not (masked == "own"):
            arrive((KEY, VALUE), block)
        scores = dot(buf[KEY, block], buf[QUERY, z], 1, 1) * scaling
        if masked:
            scores = jnp.where(key_row + block * span < own_limit, scores, HIDDEN)
        st[block] = scores
        dp[block] = dot(buf[VALUE, block], buf[GRAD, z], 1, 1)
        top[...] = jnp.maximum(top[...], jnp.max(scores, axis=0, keepdims=True))

    score(z, "own")
    @pl.when(ahead)
    def _():
        score(z + 1, "ahead")

    @pl.loop(1, z + 1)
    def _(back):
        score(z - back, None)

    last = z + ahead.astype(jnp.int32) + 1
    highest = top[...]

    def total(block, carry):
        sums, dots = carry
        probs = jnp.exp(st[block] - highest)
        st[block] = probs
        return (sums + jnp.sum(probs, axis=0, keepdims=True),
                dots + jnp.sum(probs * dp[block], axis=0, keepdims=True))

    zero = jnp.zeros_like(highest)
    sums, dots = lax.fori_loop(0, last, total, (zero, zero))
    row_dot = dots / sums
    inverse = 1.0 / sums
    stats[z, 0:1] = highest + jnp.log(sums)
    stats[z, 1:2] = row_dot
    for target in range(blocks):
        @pl.when(needed(z, target) & (z != target))
        def _():
            stat_copy(target).start()

    def key_score(block, masked):
        if masked:
            for array in (QUERY, GRAD):
                arrive_direct(array, block)
        else:
            arrive((QUERY, GRAD), block)
        scores = dot(buf[KEY, z], buf[QUERY, block], 1, 1) * scaling
        if masked:
            scores = jnp.where(key_row + z * span < limits(block, HEADS), scores, HIDDEN)
        st_key[block] = scores
        dp_key[block] = dot(buf[VALUE, z], buf[GRAD, block], 1, 1)

    @pl.when(behind)
    def _():
        key_score(z - 1, True)

    @pl.loop(z + 1, blocks)
    def _(block):
        key_score(block, False)

    def own_query(block):
        probs = st[block] * inverse
        score_grad = (probs * (dp[block] - row_dot)).astype(jnp.bfloat16)
        return probs.astype(jnp.bfloat16), score_grad

    probs, score_grad = own_query(z)
    acc_o[...] = dot(probs, buf[VALUE, z], 0, 0)
    acc_q[...] = dot(score_grad, buf[KEY, z], 0, 0)
    acc_v[...] = dot(probs, buf[GRAD, z], 1, 0)
    acc_k[...] = dot(score_grad, buf[QUERY, z], 1, 0)

    def add_query(block):
        probs, score_grad = own_query(block)
        acc_o[...] += dot(probs, buf[VALUE, block], 0, 0)
        acc_q[...] += dot(score_grad, buf[KEY, block], 0, 0)

    @pl.when(ahead)
    def _():
        add_query(z + 1)

    @pl.loop(1, z + 1)
    def _(back):
        add_query(z - back)

    res_out[0] = acc_o[other_rows, :].astype(jnp.bfloat16)
    result_copy(0).start()
    res_out[1] = (acc_q[other_rows, :] * scaling).astype(jnp.bfloat16)
    result_copy(1).start()

    def add_key(block):
        pltpu.make_async_copy(stats.at[block], stats.at[block], stat_recv.at[block]).wait()
        probs = jnp.exp(st_key[block] - stats[block, 0:1])
        score_grad = (probs * (dp_key[block] - stats[block, 1:2])).astype(jnp.bfloat16)
        acc_v[...] += dot(probs.astype(jnp.bfloat16), buf[GRAD, block], 1, 0)
        acc_k[...] += dot(score_grad, buf[QUERY, block], 1, 0)

    @pl.when(behind)
    def _():
        add_key(z - 1)

    @pl.loop(z + 1, blocks)
    def _(block):
        add_key(block)

    res_out[2] = (acc_k[other_rows, :] * scaling).astype(jnp.bfloat16)
    result_copy(2).start()
    res_out[3] = acc_v[other_rows, :].astype(jnp.bfloat16)
    result_copy(3).start()

    o_ref[:, own_columns] = acc_o[own_rows, :].astype(jnp.bfloat16)
    dq_ref[:, own_columns] = acc_q[own_rows, :] * scaling
    dk_ref[:, own_columns] = acc_k[own_rows, :] * scaling
    dv_ref[:, own_columns] = acc_v[own_rows, :]
    for slot, ref in enumerate((o_ref, dq_ref, dk_ref, dv_ref)):
        result_copy(slot).wait_recv()
        ref[:, other_columns] = res_in[slot].astype(ref.dtype)

    for slot in range(4):
        result_copy(slot).wait_send()
    limit_copy(0, 0, 0).wait_send()
    @pl.when(ahead)
    def _():
        for head in range(HEADS):
            limit_copy(0, 0, 1 + head).wait_send()
    for target in range(blocks):
        @pl.when(needed(z, target) & (z != target))
        def _():
            stat_copy(target).wait_send()
    for array, target, head, wanted in routes:
        @pl.when(wanted)
        def _():
            block_copy(array, target, head).wait_send()
    for arrays in ((KEY, VALUE), (QUERY, GRAD)):
        for block in range(blocks):
            @pl.when(forwards(arrays[0], block))
            def _():
                for array in arrays:
                    forward_copy(array, block).wait_send()


def solution(mesh):
    n = mesh.shape["ctx"]

    def local(queries, keys, values, out_grad, span_end):
        rows = queries.shape[0]
        blocks, span = n // HEADS, HEADS * rows
        f32, bf16 = jnp.float32, jnp.bfloat16
        anywhere = pl.BlockSpec(memory_space=pl.ANY)
        vmem = pl.BlockSpec(memory_space=pltpu.VMEM)
        dma = pltpu.SemaphoreType.DMA
        return pl.pallas_call(
            functools.partial(kernel, n, rows),
            out_shape=tuple(
                jax.ShapeDtypeStruct(queries.shape, kind) for kind in (bf16, f32, f32, f32)),
            in_specs=[anywhere] * 5,
            out_specs=(vmem,) * 4,
            scratch_shapes=[
                pltpu.VMEM((4, blocks, span, HEAD_DIM), bf16),
                pltpu.VMEM((2 * HEADS, 1, rows), jnp.int32),
                pltpu.VMEM((blocks, span, span), f32),
                pltpu.VMEM((blocks, span, span), f32),
                pltpu.VMEM((blocks, span, span), f32),
                pltpu.VMEM((blocks, span, span), f32),
                pltpu.VMEM((blocks, 2, span), f32),
                pltpu.VMEM((1, span), f32),
                pltpu.VMEM((span, HEAD_DIM), f32),
                pltpu.VMEM((span, HEAD_DIM), f32),
                pltpu.VMEM((span, HEAD_DIM), f32),
                pltpu.VMEM((span, HEAD_DIM), f32),
                pltpu.VMEM((4, rows, HEAD_DIM), bf16),
                pltpu.VMEM((4, rows, HEAD_DIM), bf16),
                dma((4, blocks, HEADS)),
                dma((4, blocks, HEADS)),
                dma((3,)),
                dma((2 * HEADS,)),
                dma((blocks,)),
                dma((blocks,)),
                dma((4,)),
                dma((4,)),
                dma((4, blocks)),
                dma((4, blocks)),
            ],
            compiler_params=pltpu.CompilerParams(collective_id=0, has_side_effects=True),
        )(queries, keys, values, out_grad, span_end[None])

    spec = P(("dp", "ctx"), None)
    return jax.shard_map(
        local, mesh=mesh, in_specs=(spec,) * 4 + (P(("dp", "ctx")),),
        out_specs=(spec,) * 4, check_vma=False)
```

```python
import functools

import jax
import jax.numpy as jnp
from jax import lax
from jax.experimental import pallas as pl
from jax.experimental.pallas import tpu as pltpu
from jax.sharding import PartitionSpec as P

HEADS = 2
HEAD_DIM = 128
IMG = 288
DIRECT = 2
HIDDEN = -1e30
KEY, VALUE, QUERY, GRAD = range(4)


def dot(a, b, a_dim, b_dim):
    return lax.dot_general(a, b, (((a_dim,), (b_dim,)), ((), ())), preferred_element_type=jnp.float32)


def kernel(
    n, rows,
    q_in, k_in, v_in, g_in, ends_in,
    o_ref, dq_ref, dk_ref, dv_ref,
    buf, ends, st, dp, st_key, dp_key, stats, top, acc_o, acc_q, acc_k, acc_v, res_out, res_in,
    send_sem, recv_sem, lim_send, lim_recv, stat_send, stat_recv, res_send, res_recv, pass_send, pass_recv,
):
    scaling = HEAD_DIM ** -0.5
    blocks = n // HEADS
    span = HEADS * rows
    cut = blocks * span - IMG
    me = lax.axis_index("ctx")
    z = me // HEADS
    x = me % HEADS
    sources = (k_in, v_in, q_in, g_in)

    def device(index):
        return {"ctx": index}

    def needed(query_block, key_block):
        return (
            (key_block <= query_block)
            | ((query_block + 1) * span > cut)
            | ((key_block <= query_block + 1) & (key_block * span < cut))
        )

    ahead = (z + 1 < blocks) & needed(z, z + 1)
    behind = (z > 0) & needed(z - 1, z)

    barrier = pltpu.get_barrier_semaphore()
    def close(target):
        return (target - z <= DIRECT) & (z - target <= DIRECT)

    met = -1
    for target in range(blocks):
        met = met + HEADS * close(target).astype(jnp.int32)
        for head in range(HEADS):
            @pl.when(close(target) & (target * HEADS + head != me))
            def _():
                pl.semaphore_signal(barrier, inc=1, device_id=device(target * HEADS + head))

    own_rows = pl.ds(pl.multiple_of(x * rows, 16), rows)
    other_rows = pl.ds(pl.multiple_of((1 - x) * rows, 16), rows)

    own_columns = pl.ds(pl.multiple_of(x * HEAD_DIM, HEAD_DIM), HEAD_DIM)
    other_columns = pl.ds(pl.multiple_of((1 - x) * HEAD_DIM, HEAD_DIM), HEAD_DIM)

    def limit_copy(slot, target, send):
        return pltpu.make_async_remote_copy(
            src_ref=ends_in, dst_ref=ends.at[slot], send_sem=lim_send.at[send],
            recv_sem=lim_recv.at[slot], device_id=device(target))

    def own_limit_copy():
        return pltpu.make_async_copy(ends_in, ends.at[x], lim_recv.at[x])

    def limits(block, slot):
        for portion in range(HEADS):
            ref = ends.at[slot + portion]
            pltpu.make_async_copy(ref, ref, lim_recv.at[slot + portion]).wait()
        joined = jnp.concatenate([ends[slot + portion] for portion in range(HEADS)], axis=1)
        position = lax.broadcasted_iota(jnp.int32, (1, span), 1) + block * span
        return jnp.maximum(position + 1, joined)

    def block_copy(array, target, head):
        return pltpu.make_async_remote_copy(
            src_ref=sources[array].at[:, pl.ds(head * HEAD_DIM, HEAD_DIM)],
            dst_ref=buf.at[array, z, own_rows],
            send_sem=send_sem.at[array, target, head],
            recv_sem=recv_sem.at[array, z, x],
            device_id=device(target * HEADS + head))

    def local_copy(array):
        return pltpu.make_async_copy(
            sources[array].at[:, own_columns],
            buf.at[array, z, own_rows],
            recv_sem.at[array, z, x])

    def stat_copy(target):
        return pltpu.make_async_remote_copy(
            src_ref=stats.at[z], dst_ref=stats.at[z], send_sem=stat_send.at[target],
            recv_sem=stat_recv.at[z], device_id=device(target * HEADS + x))

    def result_copy(slot):
        return pltpu.make_async_remote_copy(
            src_ref=res_out.at[slot], dst_ref=res_in.at[slot], send_sem=res_send.at[slot],
            recv_sem=res_recv.at[slot], device_id=device(z * HEADS + 1 - x))

    own_limit_copy().start()
    for array in range(4):
        local_copy(array).start()
    pl.semaphore_wait(barrier, met)

    limit_copy(x, z * HEADS + 1 - x, 0).start()
    @pl.when(ahead)
    def _():
        for head in range(HEADS):
            limit_copy(HEADS + x, (z + 1) * HEADS + head, 1 + head).start()

    routes = []
    for step in range(blocks):
        for array, target in (
            (KEY, blocks - 1 - step), (VALUE, blocks - 1 - step), (QUERY, step), (GRAD, step)):
            wanted = needed(target, z) if array in (KEY, VALUE) else needed(z, target)
            near = close(target)
            for head in range(HEADS):
                away = target * HEADS + head != me
                routes.append((array, target, head, wanted & near & away))
    for array, target, head, wanted in routes:
        @pl.when(wanted)
        def _():
            block_copy(array, target, head).start()

    def forward_copy(array, block):
        target = z + 1 if array in (KEY, VALUE) else z - 1
        return pltpu.make_async_remote_copy(
            src_ref=buf.at[array, block], dst_ref=buf.at[array, block],
            send_sem=pass_send.at[array, block], recv_sem=pass_recv.at[array, block],
            device_id=device(target * HEADS + x))

    def forwards(array, block):
        if array in (KEY, VALUE):
            return (z - block >= DIRECT) & (z + 1 < blocks)
        return (block - z >= DIRECT) & (z > 0)

    def arrive_direct(array, block):
        for portion in range(HEADS):
            ref = buf.at[array, block, pl.ds(portion * rows, rows)]
            pltpu.make_async_copy(ref, ref, recv_sem.at[array, block, portion]).wait()

    def arrive_forwarded(array, block):
        ref = buf.at[array, block]
        pltpu.make_async_copy(ref, ref, pass_recv.at[array, block]).wait()

    def relay(arrays, block):
        @pl.when(forwards(arrays[0], block))
        def _():
            for array in arrays:
                @pl.when(close(block))
                def _():
                    arrive_direct(array, block)
                @pl.when(jnp.logical_not(close(block)))
                def _():
                    arrive_forwarded(array, block)
                forward_copy(array, block).start()

    def arrive(arrays, block):
        held = forwards(arrays[0], block)
        @pl.when(close(block) & jnp.logical_not(held))
        def _():
            for array in arrays:
                arrive_direct(array, block)
        @pl.when(jnp.logical_not(close(block) | held))
        def _():
            for array in arrays:
                arrive_forwarded(array, block)

    for array in (KEY, QUERY, VALUE, GRAD):
        arrive_direct(array, z)
    own_limit = limits(z, 0)
    key_row = lax.broadcasted_iota(jnp.int32, (span, span), 0)
    top[...] = jnp.full_like(top, HIDDEN)

    def score(block, masked):
        if not (masked == "own"):
            arrive((KEY, VALUE), block)
        scores = dot(buf[KEY, block], buf[QUERY, z], 1, 1) * scaling
        if masked:
            scores = jnp.where(key_row + block * span < own_limit, scores, HIDDEN)
        st[block] = scores
        dp[block] = dot(buf[VALUE, block], buf[GRAD, z], 1, 1)
        top[...] = jnp.maximum(top[...], jnp.max(scores, axis=0, keepdims=True))

    score(z, "own")

    @pl.loop(0, blocks)
    def _(block):
        relay((KEY, VALUE), block)
        relay((QUERY, GRAD), block)

    @pl.when(ahead)
    def _():
        score(z + 1, "ahead")

    @pl.loop(1, z + 1)
    def _(back):
        score(z - back, None)

    last = z + ahead.astype(jnp.int32) + 1
    highest = top[...]

    def total(block, carry):
        sums, dots = carry
        probs = jnp.exp(st[block] - highest)
        st[block] = probs
        return (sums + jnp.sum(probs, axis=0, keepdims=True),
                dots + jnp.sum(probs * dp[block], axis=0, keepdims=True))

    zero = jnp.zeros_like(highest)
    sums, dots = lax.fori_loop(0, last, total, (zero, zero))
    row_dot = dots / sums
    inverse = 1.0 / sums
    stats[z, 0:1] = highest + jnp.log(sums)
    stats[z, 1:2] = row_dot
    for target in range(blocks):
        @pl.when(needed(z, target) & (z != target))
        def _():
            stat_copy(target).start()

    def own_query(block):
        probs = st[block] * inverse
        score_grad = (probs * (dp[block] - row_dot)).astype(jnp.bfloat16)
        return probs.astype(jnp.bfloat16), score_grad

    probs, score_grad = own_query(z)
    acc_o[...] = dot(probs, buf[VALUE, z], 0, 0)
    acc_q[...] = dot(score_grad, buf[KEY, z], 0, 0)
    acc_v[...] = dot(probs, buf[GRAD, z], 1, 0)
    acc_k[...] = dot(score_grad, buf[QUERY, z], 1, 0)

    def add_query(block):
        probs, score_grad = own_query(block)
        acc_o[...] += dot(probs, buf[VALUE, block], 0, 0)
        acc_q[...] += dot(score_grad, buf[KEY, block], 0, 0)

    @pl.when(ahead)
    def _():
        add_query(z + 1)

    @pl.loop(1, z + 1)
    def _(back):
        add_query(z - back)

    res_out[0] = acc_o[other_rows, :].astype(jnp.bfloat16)
    result_copy(0).start()
    res_out[1] = (acc_q[other_rows, :] * scaling).astype(jnp.bfloat16)
    result_copy(1).start()

    def key_score(block, masked):
        if masked:
            for array in (QUERY, GRAD):
                arrive_direct(array, block)
        else:
            arrive((QUERY, GRAD), block)
        scores = dot(buf[KEY, z], buf[QUERY, block], 1, 1) * scaling
        if masked:
            scores = jnp.where(key_row + z * span < limits(block, HEADS), scores, HIDDEN)
        st_key[block] = scores
        dp_key[block] = dot(buf[VALUE, z], buf[GRAD, block], 1, 1)

    @pl.when(behind)
    def _():
        key_score(z - 1, True)

    @pl.loop(z + 1, blocks)
    def _(block):
        key_score(block, False)

    def add_value(block):
        pltpu.make_async_copy(stats.at[block], stats.at[block], stat_recv.at[block]).wait()
        probs = jnp.exp(st_key[block] - stats[block, 0:1])
        acc_v[...] += dot(probs.astype(jnp.bfloat16), buf[GRAD, block], 1, 0)
        st_key[block] = probs

    def add_key(block):
        score_grad = (st_key[block] * (dp_key[block] - stats[block, 1:2])).astype(jnp.bfloat16)
        acc_k[...] += dot(score_grad, buf[QUERY, block], 1, 0)

    for step in (add_value, add_key):
        @pl.when(behind)
        def _():
            step(z - 1)

        @pl.loop(z + 1, blocks)
        def _(block):
            step(block)

        if step is add_value:
            res_out[3] = acc_v[other_rows, :].astype(jnp.bfloat16)
            result_copy(3).start()
        else:
            res_out[2] = (acc_k[other_rows, :] * scaling).astype(jnp.bfloat16)
            result_copy(2).start()

    o_ref[:, own_columns] = acc_o[own_rows, :].astype(jnp.bfloat16)
    dq_ref[:, own_columns] = acc_q[own_rows, :] * scaling
    dk_ref[:, own_columns] = acc_k[own_rows, :] * scaling
    dv_ref[:, own_columns] = acc_v[own_rows, :]
    for slot, ref in ((0, o_ref), (1, dq_ref), (3, dv_ref), (2, dk_ref)):
        result_copy(slot).wait_recv()
        ref[:, other_columns] = res_in[slot].astype(ref.dtype)

    for slot in range(4):
        result_copy(slot).wait_send()
    limit_copy(0, 0, 0).wait_send()
    @pl.when(ahead)
    def _():
        for head in range(HEADS):
            limit_copy(0, 0, 1 + head).wait_send()
    for target in range(blocks):
        @pl.when(needed(z, target) & (z != target))
        def _():
            stat_copy(target).wait_send()
    for array, target, head, wanted in routes:
        @pl.when(wanted)
        def _():
            block_copy(array, target, head).wait_send()
    for arrays in ((KEY, VALUE), (QUERY, GRAD)):
        for block in range(blocks):
            @pl.when(forwards(arrays[0], block))
            def _():
                for array in arrays:
                    forward_copy(array, block).wait_send()


def flush(*refs):
    sem = refs[-1]
    copies = [pltpu.make_async_copy(refs[i], refs[i + 4], sem.at[i]) for i in range(4)]
    for copy in copies:
        copy.start()
    for copy in copies:
        copy.wait()


def solution(mesh):
    n = mesh.shape["ctx"]

    def local(queries, keys, values, out_grad, span_end):
        rows = queries.shape[0]
        blocks, span = n // HEADS, HEADS * rows
        f32, bf16 = jnp.float32, jnp.bfloat16
        anywhere = pl.BlockSpec(memory_space=pl.ANY)
        vmem = pl.BlockSpec(memory_space=pltpu.VMEM)
        dma = pltpu.SemaphoreType.DMA
        results = pl.pallas_call(
            functools.partial(kernel, n, rows),
            out_shape=tuple(
                pltpu.VMEM(queries.shape, kind) for kind in (bf16, f32, f32, f32)),
            in_specs=[anywhere] * 5,
            out_specs=(vmem,) * 4,
            scratch_shapes=[
                pltpu.VMEM((4, blocks, span, HEAD_DIM), bf16),
                pltpu.VMEM((2 * HEADS, 1, rows), jnp.int32),
                pltpu.VMEM((blocks, span, span), f32),
                pltpu.VMEM((blocks, span, span), f32),
                pltpu.VMEM((blocks, span, span), f32),
                pltpu.VMEM((blocks, span, span), f32),
                pltpu.VMEM((blocks, 2, span), f32),
                pltpu.VMEM((1, span), f32),
                pltpu.VMEM((span, HEAD_DIM), f32),
                pltpu.VMEM((span, HEAD_DIM), f32),
                pltpu.VMEM((span, HEAD_DIM), f32),
                pltpu.VMEM((span, HEAD_DIM), f32),
                pltpu.VMEM((4, rows, HEAD_DIM), bf16),
                pltpu.VMEM((4, rows, HEAD_DIM), bf16),
                dma((4, blocks, HEADS)),
                dma((4, blocks, HEADS)),
                dma((3,)),
                dma((2 * HEADS,)),
                dma((blocks,)),
                dma((blocks,)),
                dma((4,)),
                dma((4,)),
                dma((4, blocks)),
                dma((4, blocks)),
            ],
            compiler_params=pltpu.CompilerParams(collective_id=0, has_side_effects=True),
        )(queries, keys, values, out_grad, span_end[None])
        return pl.pallas_call(
            flush,
            out_shape=tuple(
                jax.ShapeDtypeStruct(queries.shape, kind) for kind in (bf16, f32, f32, f32)),
            in_specs=[vmem] * 4,
            out_specs=(anywhere,) * 4,
            scratch_shapes=[dma((4,))],
        )(*(pltpu.with_memory_space_constraint(result, pltpu.VMEM) for result in results))

    spec = P(("dp", "ctx"), None)
    return jax.shard_map(
        local, mesh=mesh, in_specs=(spec,) * 4 + (P(("dp", "ctx")),),
        out_specs=(spec,) * 4, check_vma=False)
```

```python
import functools

import jax
import jax.numpy as jnp
from jax import lax
from jax.experimental import pallas as pl
from jax.experimental.pallas import tpu as pltpu
from jax.sharding import PartitionSpec as P

HEADS = 2
HEAD_DIM = 128
IMG = 288
DIRECT = 2
HIDDEN = -1e30
KEY, VALUE, QUERY, GRAD = range(4)


def dot(a, b, a_dim, b_dim):
    return lax.dot_general(a, b, (((a_dim,), (b_dim,)), ((), ())), preferred_element_type=jnp.float32)


def kernel(
    n, rows,
    q_in, k_in, v_in, g_in, ends_in,
    o_ref, dq_ref, dk_ref, dv_ref,
    buf, ends, st, dp, st_key, dp_key, stats, top, acc_o, acc_q, acc_k, acc_v, res_out, res_in,
    send_sem, recv_sem, lim_send, lim_recv, stat_send, stat_recv, res_send, res_recv, pass_send, pass_recv,
):
    scaling = HEAD_DIM ** -0.5
    blocks = n // HEADS
    span = HEADS * rows
    cut = blocks * span - IMG
    me = lax.axis_index("ctx")
    z = me // HEADS
    x = me % HEADS
    sources = (k_in, v_in, q_in, g_in)

    def device(index):
        return {"ctx": index}

    def needed(query_block, key_block):
        return (
            (key_block <= query_block)
            | ((query_block + 1) * span > cut)
            | ((key_block <= query_block + 1) & (key_block * span < cut))
        )

    ahead = (z + 1 < blocks) & needed(z, z + 1)
    behind = (z > 0) & needed(z - 1, z)

    barrier = pltpu.get_barrier_semaphore()
    def close(target):
        return (target - z <= DIRECT) & (z - target <= DIRECT)

    met = -1
    for target in range(blocks):
        met = met + HEADS * close(target).astype(jnp.int32)
        for head in range(HEADS):
            @pl.when(close(target) & (target * HEADS + head != me))
            def _():
                pl.semaphore_signal(barrier, inc=1, device_id=device(target * HEADS + head))

    own_rows = pl.ds(pl.multiple_of(x * rows, 16), rows)
    other_rows = pl.ds(pl.multiple_of((1 - x) * rows, 16), rows)

    own_columns = pl.ds(pl.multiple_of(x * HEAD_DIM, HEAD_DIM), HEAD_DIM)
    other_columns = pl.ds(pl.multiple_of((1 - x) * HEAD_DIM, HEAD_DIM), HEAD_DIM)

    def limit_copy(slot, target, send):
        return pltpu.make_async_remote_copy(
            src_ref=ends_in, dst_ref=ends.at[slot], send_sem=lim_send.at[send],
            recv_sem=lim_recv.at[slot], device_id=device(target))

    def own_limit_copy():
        return pltpu.make_async_copy(ends_in, ends.at[x], lim_recv.at[x])

    def limits(block, slot):
        for portion in range(HEADS):
            ref = ends.at[slot + portion]
            pltpu.make_async_copy(ref, ref, lim_recv.at[slot + portion]).wait()
        joined = jnp.concatenate([ends[slot + portion] for portion in range(HEADS)], axis=1)
        position = lax.broadcasted_iota(jnp.int32, (1, span), 1) + block * span
        return jnp.maximum(position + 1, joined)

    def block_copy(array, target, head):
        return pltpu.make_async_remote_copy(
            src_ref=sources[array].at[:, pl.ds(head * HEAD_DIM, HEAD_DIM)],
            dst_ref=buf.at[array, z, own_rows],
            send_sem=send_sem.at[array, target, head],
            recv_sem=recv_sem.at[array, z, x],
            device_id=device(target * HEADS + head))

    def local_copy(array):
        return pltpu.make_async_copy(
            sources[array].at[:, own_columns],
            buf.at[array, z, own_rows],
            recv_sem.at[array, z, x])

    def stat_copy(target):
        return pltpu.make_async_remote_copy(
            src_ref=stats.at[z], dst_ref=stats.at[z], send_sem=stat_send.at[target],
            recv_sem=stat_recv.at[z], device_id=device(target * HEADS + x))

    def result_copy(slot):
        return pltpu.make_async_remote_copy(
            src_ref=res_out.at[slot], dst_ref=res_in.at[slot], send_sem=res_send.at[slot],
            recv_sem=res_recv.at[slot], device_id=device(z * HEADS + 1 - x))

    own_limit_copy().start()
    for array in range(4):
        local_copy(array).start()
    pl.semaphore_wait(barrier, met)

    limit_copy(x, z * HEADS + 1 - x, 0).start()
    @pl.when(ahead)
    def _():
        for head in range(HEADS):
            limit_copy(HEADS + x, (z + 1) * HEADS + head, 1 + head).start()

    routes = []
    order = [(array, blocks - 1 - step) for step in range(blocks) for array in (KEY, VALUE)]
    order += [(array, step) for step in range(blocks) for array in (QUERY, GRAD)]
    for array, target in order:
        wanted = needed(target, z) if array in (KEY, VALUE) else needed(z, target)
        near = close(target)
        for head in range(HEADS):
            away = target * HEADS + head != me
            routes.append((array, target, head, wanted & near & away))
    for array, target, head, wanted in routes:
        @pl.when(wanted)
        def _():
            block_copy(array, target, head).start()

    def forward_copy(array, block):
        target = z + 1 if array in (KEY, VALUE) else z - 1
        return pltpu.make_async_remote_copy(
            src_ref=buf.at[array, block], dst_ref=buf.at[array, block],
            send_sem=pass_send.at[array, block], recv_sem=pass_recv.at[array, block],
            device_id=device(target * HEADS + x))

    def forwards(array, block):
        if array in (KEY, VALUE):
            return (z - block >= DIRECT) & (z + 1 < blocks)
        return (block - z >= DIRECT) & (z > 0)

    def arrive_direct(array, block):
        for portion in range(HEADS):
            ref = buf.at[array, block, pl.ds(portion * rows, rows)]
            pltpu.make_async_copy(ref, ref, recv_sem.at[array, block, portion]).wait()

    def arrive_forwarded(array, block):
        ref = buf.at[array, block]
        pltpu.make_async_copy(ref, ref, pass_recv.at[array, block]).wait()

    def relay(arrays, block):
        @pl.when(forwards(arrays[0], block))
        def _():
            for array in arrays:
                @pl.when(close(block))
                def _():
                    arrive_direct(array, block)
                @pl.when(jnp.logical_not(close(block)))
                def _():
                    arrive_forwarded(array, block)
                forward_copy(array, block).start()

    def arrive(arrays, block):
        held = forwards(arrays[0], block)
        @pl.when(close(block) & jnp.logical_not(held))
        def _():
            for array in arrays:
                arrive_direct(array, block)
        @pl.when(jnp.logical_not(close(block) | held))
        def _():
            for array in arrays:
                arrive_forwarded(array, block)

    @pl.loop(0, blocks)
    def _(block):
        relay((KEY, VALUE), block)
        relay((QUERY, GRAD), block)

    for array in (KEY, QUERY, VALUE, GRAD):
        arrive_direct(array, z)
    own_limit = limits(z, 0)
    key_row = lax.broadcasted_iota(jnp.int32, (span, span), 0)
    top[0:1] = jnp.full((1, span), HIDDEN, jnp.float32)
    top[1:3] = jnp.zeros((2, span), jnp.float32)

    def score(block, masked):
        if not (masked == "own"):
            arrive((KEY, VALUE), block)
        scores = dot(buf[KEY, block], buf[QUERY, z], 1, 1) * scaling
        if masked:
            scores = jnp.where(key_row + block * span < own_limit, scores, HIDDEN)
        st[block] = scores
        prob_grad = dot(buf[VALUE, block], buf[GRAD, z], 1, 1)
        dp[block] = prob_grad
        highest = jnp.maximum(top[0:1], jnp.max(scores, axis=0, keepdims=True))
        probs = jnp.exp(scores - highest)
        factor = jnp.exp(top[0:1] - highest)
        top[0:1] = highest
        top[1:2] = top[1:2] * factor + jnp.sum(probs, axis=0, keepdims=True)
        top[2:3] = top[2:3] * factor + jnp.sum(probs * prob_grad, axis=0, keepdims=True)

    score(z, "own")

    @pl.when(ahead)
    def _():
        score(z + 1, "ahead")

    @pl.loop(1, z + 1)
    def _(back):
        score(z - back, None)

    log_total = top[0:1] + jnp.log(top[1:2])
    row_dot = top[2:3] / top[1:2]
    stats[z, 0:1] = log_total
    stats[z, 1:2] = row_dot
    for target in range(blocks):
        @pl.when(needed(z, target) & (z != target))
        def _():
            stat_copy(target).start()

    def own_query(block):
        probs = jnp.exp(st[block] - log_total)
        score_grad = (probs * (dp[block] - row_dot)).astype(jnp.bfloat16)
        return probs.astype(jnp.bfloat16), score_grad

    probs, score_grad = own_query(z)
    acc_o[...] = dot(probs, buf[VALUE, z], 0, 0)
    acc_q[...] = dot(score_grad, buf[KEY, z], 0, 0)
    acc_v[...] = dot(probs, buf[GRAD, z], 1, 0)
    acc_k[...] = dot(score_grad, buf[QUERY, z], 1, 0)

    def add_query(block):
        probs, score_grad = own_query(block)
        acc_o[...] += dot(probs, buf[VALUE, block], 0, 0)
        acc_q[...] += dot(score_grad, buf[KEY, block], 0, 0)

    @pl.when(ahead)
    def _():
        add_query(z + 1)

    @pl.loop(1, z + 1)
    def _(back):
        add_query(z - back)

    res_out[0] = acc_o[other_rows, :].astype(jnp.bfloat16)
    result_copy(0).start()
    res_out[1] = (acc_q[other_rows, :] * scaling).astype(jnp.bfloat16)
    result_copy(1).start()

    def key_score(block, masked):
        if masked:
            for array in (QUERY, GRAD):
                arrive_direct(array, block)
        else:
            arrive((QUERY, GRAD), block)
        scores = dot(buf[KEY, z], buf[QUERY, block], 1, 1) * scaling
        if masked:
            scores = jnp.where(key_row + z * span < limits(block, HEADS), scores, HIDDEN)
        st_key[block] = scores
        dp_key[block] = dot(buf[VALUE, z], buf[GRAD, block], 1, 1)

    @pl.when(behind)
    def _():
        key_score(z - 1, True)

    @pl.loop(z + 1, blocks)
    def _(block):
        key_score(block, False)

    def arrive_stats(block):
        pltpu.make_async_copy(stats.at[block], stats.at[block], stat_recv.at[block]).wait()

    def add_key(block, part):
        probs = jnp.exp(st_key[block, part] - stats[block, 0:1])
        acc_v[part] += dot(probs.astype(jnp.bfloat16), buf[GRAD, block], 1, 0)
        score_grad = (probs * (dp_key[block, part] - stats[block, 1:2])).astype(jnp.bfloat16)
        acc_k[part] += dot(score_grad, buf[QUERY, block], 1, 0)

    @pl.when(behind)
    def _():
        arrive_stats(z - 1)
        add_key(z - 1, slice(None))

    @pl.loop(z + 1, blocks - 1)
    def _(block):
        arrive_stats(block)
        add_key(block, slice(None))

    @pl.when(z < blocks - 1)
    def _():
        arrive_stats(blocks - 1)
        add_key(blocks - 1, other_rows)

    res_out[3] = acc_v[other_rows, :].astype(jnp.bfloat16)
    result_copy(3).start()
    res_out[2] = (acc_k[other_rows, :] * scaling).astype(jnp.bfloat16)
    result_copy(2).start()

    @pl.when(z < blocks - 1)
    def _():
        add_key(blocks - 1, own_rows)

    o_ref[:, own_columns] = acc_o[own_rows, :].astype(jnp.bfloat16)
    dq_ref[:, own_columns] = acc_q[own_rows, :] * scaling
    dk_ref[:, own_columns] = acc_k[own_rows, :] * scaling
    dv_ref[:, own_columns] = acc_v[own_rows, :]
    for slot, ref in ((0, o_ref), (1, dq_ref), (3, dv_ref), (2, dk_ref)):
        result_copy(slot).wait_recv()
        ref[:, other_columns] = res_in[slot].astype(ref.dtype)

    for slot in range(4):
        result_copy(slot).wait_send()
    limit_copy(0, 0, 0).wait_send()
    @pl.when(ahead)
    def _():
        for head in range(HEADS):
            limit_copy(0, 0, 1 + head).wait_send()
    for target in range(blocks):
        @pl.when(needed(z, target) & (z != target))
        def _():
            stat_copy(target).wait_send()
    for array, target, head, wanted in routes:
        @pl.when(wanted)
        def _():
            block_copy(array, target, head).wait_send()
    for arrays in ((KEY, VALUE), (QUERY, GRAD)):
        for block in range(blocks):
            @pl.when(forwards(arrays[0], block))
            def _():
                for array in arrays:
                    forward_copy(array, block).wait_send()


def flush(*refs):
    sem = refs[-1]
    copies = [pltpu.make_async_copy(refs[i], refs[i + 4], sem.at[i]) for i in range(4)]
    for copy in copies:
        copy.start()
    for copy in copies:
        copy.wait()


def solution(mesh):
    n = mesh.shape["ctx"]

    def local(queries, keys, values, out_grad, span_end):
        rows = queries.shape[0]
        blocks, span = n // HEADS, HEADS * rows
        f32, bf16 = jnp.float32, jnp.bfloat16
        anywhere = pl.BlockSpec(memory_space=pl.ANY)
        vmem = pl.BlockSpec(memory_space=pltpu.VMEM)
        dma = pltpu.SemaphoreType.DMA
        results = pl.pallas_call(
            functools.partial(kernel, n, rows),
            out_shape=tuple(
                pltpu.VMEM(queries.shape, kind) for kind in (bf16, f32, f32, f32)),
            in_specs=[anywhere] * 5,
            out_specs=(vmem,) * 4,
            scratch_shapes=[
                pltpu.VMEM((4, blocks, span, HEAD_DIM), bf16),
                pltpu.VMEM((2 * HEADS, 1, rows), jnp.int32),
                pltpu.VMEM((blocks, span, span), f32),
                pltpu.VMEM((blocks, span, span), f32),
                pltpu.VMEM((blocks, span, span), f32),
                pltpu.VMEM((blocks, span, span), f32),
                pltpu.VMEM((blocks, 2, span), f32),
                pltpu.VMEM((3, span), f32),
                pltpu.VMEM((span, HEAD_DIM), f32),
                pltpu.VMEM((span, HEAD_DIM), f32),
                pltpu.VMEM((span, HEAD_DIM), f32),
                pltpu.VMEM((span, HEAD_DIM), f32),
                pltpu.VMEM((4, rows, HEAD_DIM), bf16),
                pltpu.VMEM((4, rows, HEAD_DIM), bf16),
                dma((4, blocks, HEADS)),
                dma((4, blocks, HEADS)),
                dma((3,)),
                dma((2 * HEADS,)),
                dma((blocks,)),
                dma((blocks,)),
                dma((4,)),
                dma((4,)),
                dma((4, blocks)),
                dma((4, blocks)),
            ],
            compiler_params=pltpu.CompilerParams(collective_id=0, has_side_effects=True),
        )(queries, keys, values, out_grad, span_end[None])
        return pl.pallas_call(
            flush,
            out_shape=tuple(
                jax.ShapeDtypeStruct(queries.shape, kind) for kind in (bf16, f32, f32, f32)),
            in_specs=[vmem] * 4,
            out_specs=(anywhere,) * 4,
            scratch_shapes=[dma((4,))],
        )(*(pltpu.with_memory_space_constraint(result, pltpu.VMEM) for result in results))

    spec = P(("dp", "ctx"), None)
    return jax.shard_map(
        local, mesh=mesh, in_specs=(spec,) * 4 + (P(("dp", "ctx")),),
        out_specs=(spec,) * 4, check_vma=False)
```
